128 devices in a mesh: region: 8 (over x, core), tile: 16 (over z, y).
Axes of the slice: x: 4, y: 4, z: 4, core: 2. Of those that a mesh axis runs over, the one named last changes fastest.
Arguments:
- coefficients: bfloat16 [131072, 145], P(('region', 'tile')), may hold values from 0.0009994507 to 0.019897461
- peak_power: bfloat16 [131072], P(('region', 'tile')), may hold values from 0.5 to 4
- inverter_limit: bfloat16 [131072], P(('region', 'tile')), may hold values from 0.5 to 3
- building_feeder: int32 [131072, 1], P(('region', 'tile')), may hold values from 0 to 127; in each aligned block of 1024 rows (0 to 1023, 1024 to 2047, ...) at most 16 rows name the same one
- building_node: int32 [131072], P(('region', 'tile')), may hold values from 0 to 2047
- sky_radiance: bfloat16 [145, 768], replicated, may hold values from 0.0099487305 to 10
- feeder_nodes: int32 [128], P(('region', 'tile')), may hold values from 1 to 2048, 163840 in all
- sensitivity: bfloat16 [128, 2048, 2048], P(('region', 'tile')), may hold values from -0.125 to 0.125
- feeder_substation: int32 [128], P(('region', 'tile')), may hold values from 0 to 31
- mv_sensitivity: float32 [32, 32], replicated, may hold values from -1 to 1
Outputs:
- node_voltage: bfloat16 [128, 2048, 768], P(('region', 'tile'))
The draws below stay inside these ranges and needn't reach their ends.
Inputs may be any that keep to these rules, and one draw needn't show every extreme that they name: `building_feeder`: among the rows of one device no feeder is named more than 16 times, a bound that some block reaches. `feeder_nodes`: the counts sum to 128 * 2048 * 5 // 8 and the largest is exactly 2048.
All inputs are finite; a program needn't handle non-finite values. No bound on the sum of `feeder_nodes` on one device may be relied on, other than what follows from the above.
Results may differ from the reference program's by a relative error of at most 0.0006.
The reference program's roundings to bfloat16 on the way count: a program that leaves them out, or rounds other values in their place, can miss the bound.
Values may be sent and summed in bfloat16 or wider, within the bound.
A program may use at most 64 MiB of HBM per device.

```python
import math
import jax
import jax.numpy as jnp
import numpy as np
from jax import lax

P_SIZE = 145
NODES = 2048
B_DEV = 1024
COLS = 768
FEEDERS = 128
BUILDINGS = 131072
CAP = 16
SUBST = 32


def with_ends(array, rng, low, high):
    spot = [jax.random.randint(jax.random.fold_in(rng, axis), (), 0, length) for axis, length in enumerate(array.shape)]
    widest = array.shape.index(max(array.shape))
    neighbour = spot[:widest] + [(spot[widest] + 1) % array.shape[widest]] + spot[widest + 1:]
    return array.at[tuple(spot)].set(low).at[tuple(neighbour)].set(high)


def level_of(stream_key, dims, cuts, low, top_value):
    factor_of = 1.0
    for position, parts in cuts:
        heights = jax.random.uniform(jax.random.fold_in(jax.random.fold_in(stream_key, 6), position), (parts,), jnp.float32, low / len(cuts), top_value / len(cuts))
        factor_of = factor_of * jnp.repeat(jnp.exp(heights), dims[position] // parts).reshape((-1,) + (1,) * (len(dims) - 1 - position))
    return factor_of


def profile(number_of, total, reach, skew):
    weights = [(1 << 20) // math.isqrt(grade ** skew) + 1 for grade in range(2, number_of + 1)]
    spare, counts = total - reach - (number_of - 1), [1] * (number_of - 1)
    while spare > 0:
        free = [i for i in range(number_of - 1) if counts[i] < reach]
        mass, budget = sum([weights[i] for i in free]), spare
        for i in free:
            extra = min(reach - counts[i], max(1, budget * weights[i] // mass), spare)
            counts[i] = counts[i] + extra
            spare = spare - extra
    return np.array([reach] + counts)


def uneven(own_key, number_of, total, bound, lean):
    if number_of == 2:
        one = jax.random.randint(own_key, (), max(1, total - bound), min(bound, total - 1) + 1)
        return jnp.stack([one, total - one])
    lengths = jnp.asarray(profile(number_of, total, bound, lean), jnp.int32)
    pairs = (number_of - 1) // 2
    donor, taker = lengths[1:1 + 2 * pairs:2], lengths[2:2 + 2 * pairs:2]
    margin = jnp.minimum(donor - 1, bound - taker)
    moved = jax.random.randint(jax.random.fold_in(own_key, 1), (pairs,), 0, 1 << 20) % (margin + 1)
    lengths = lengths.at[1:1 + 2 * pairs:2].set(donor - moved).at[2:2 + 2 * pairs:2].set(taker + moved)
    return lengths[jax.random.permutation(jax.random.fold_in(own_key, 2), number_of)]


def shared_out(own_key, own, number, rows, count, top, limit, slope):
    sequence = jax.random.permutation(own_key, count)
    heavy_load, usual = shares(count, rows * top, limit, slope, True), shares(count, rows * top, limit, slope, False)
    places = jnp.arange(count)

    def named(sizes, turn):
        used = int((sizes > 0).sum())
        fixed = max(1, used // 4)
        passed = fixed + (places - fixed + turn * (used - fixed)) % max(1, count - fixed)
        return jnp.zeros((count,), jnp.int32).at[sequence[jnp.where(places < fixed, places, passed)]].set(jnp.asarray(sizes, jnp.int32))

    sizes = jnp.where(number % 4 == 0, named(heavy_load, number // 4), named(usual, number - number // 4 - 1))
    mixed = jax.random.permutation(jax.random.fold_in(own, 3), count)
    source_of, sink = mixed[0:count // 2 * 2:2], mixed[1:count // 2 * 2:2]
    slack = jnp.minimum(sizes[source_of] - 1, limit - sizes[sink]) // 2
    slack = jnp.where((source_of == sequence[0]) | (sink == sequence[0]) | (sizes[sink] == 0), 0, jnp.maximum(slack, 0))
    passed = jax.random.randint(jax.random.fold_in(own, 4), (count // 2,), 0, 1 << 20) % (slack + 1)
    sizes = sizes.at[source_of].add(-passed).at[sink].add(passed)
    items = jnp.searchsorted(jnp.cumsum(sizes), jnp.arange(rows * top), side="right").astype(jnp.int32)
    table = items.reshape(top, rows).T
    table = table[jax.random.permutation(jax.random.fold_in(own, 1), rows)]
    turn = jax.random.randint(jax.random.fold_in(own, 2), (rows, 1), 0, top)
    return jnp.take_along_axis(table, (jnp.arange(top)[None, :] + turn) % top, axis=1)


def shares(amount, total, reach, skew, full):
    loads = [(1 << 20) // math.isqrt(rank ** skew) + 1 for rank in range(1, amount + 1)]
    largest = reach if full else min(reach, max(-(-total // amount), total * loads[0] // sum(loads)))
    least = 1 if total - largest >= amount - 1 else 0
    holding, spare = [largest] + [least] * (amount - 1), total - largest - least * (amount - 1)
    while spare > 0:
        free = [i for i in range(1, amount) if holding[i] < largest] or [i for i in range(1, amount) if holding[i] < reach]
        pool, remaining = sum([loads[i] for i in free]), spare
        for i in free:
            more = min(reach - holding[i], max(1, remaining * loads[i] // pool), spare)
            holding[i] = holding[i] + more
            spare = spare - more
    return np.array(holding)


def noise(stream_key, extent, deviation, limit, split=(), held_as=jnp.bfloat16):
    drawn = jax.random.normal(stream_key, extent, jnp.float32) * deviation
    if len(split) > 0:
        drawn = level_of(stream_key, extent, split, -0.22, 0.18) * drawn
    return jnp.clip(drawn, min=-limit, max=limit).astype(held_as)


def setup_inputs(seed: int = 0) -> dict:
    seeds = jax.random.split(jax.random.key(seed), 11)
    coefficients = jnp.clip(jnp.exp(math.log(0.019897461) - 2.9911416 * jax.random.uniform(seeds[0], (BUILDINGS, P_SIZE), jnp.float32) ** level_of(seeds[0], (BUILDINGS, P_SIZE), ((0, 128),), -0.2, 0.2)), 0.0009994507, 0.019897461).astype(jnp.bfloat16)
    peak_power = jnp.clip(jnp.exp(math.log(4.0) - 2.0794415 * jax.random.uniform(seeds[1], (BUILDINGS,), jnp.float32) ** level_of(seeds[1], (BUILDINGS,), ((0, 128),), -0.2, 0.2)), 0.5, 4.0).astype(jnp.bfloat16)
    inverter_limit = jnp.clip(jnp.exp(math.log(3.0) - 1.7917595 * jax.random.uniform(seeds[2], (BUILDINGS,), jnp.float32) ** level_of(seeds[2], (BUILDINGS,), ((0, 128),), -0.2, 0.2)), 0.5, 3.0).astype(jnp.bfloat16)
    building_feeder_keys = jax.random.split(jax.random.fold_in(seeds[3], 1), BUILDINGS // B_DEV)
    building_feeder_turns = jax.random.permutation(jax.random.fold_in(seeds[3], 3), BUILDINGS // B_DEV)
    building_feeder = jax.vmap(lambda own, number: shared_out(jax.random.fold_in(seeds[3], 2), own, number, B_DEV, FEEDERS, 1, CAP, 2))(building_feeder_keys, building_feeder_turns).reshape((BUILDINGS, 1))
    building_node = with_ends(jax.random.randint(seeds[4], (BUILDINGS,), 0, NODES), jax.random.fold_in(seeds[4], 1), 0, NODES - 1).astype(jnp.int32)
    sky_radiance = jnp.clip(jnp.exp(jax.random.uniform(seeds[5], (P_SIZE, COLS), jnp.float32, math.log(0.0099487305), math.log(10.0))), 0.0099487305, 10.0).astype(jnp.bfloat16)
    feeder_nodes = uneven(seeds[6], FEEDERS, FEEDERS * NODES * 5 // 8, NODES, 1).astype(jnp.int32)
    sensitivity = noise(seeds[7], (FEEDERS, NODES, NODES), NODES ** -0.5, 0.125, ((0, 128),))
    feeder_substation = with_ends(jax.random.randint(seeds[8], (FEEDERS,), 0, SUBST), jax.random.fold_in(seeds[8], 1), 0, SUBST - 1).astype(jnp.int32)
    mv_sensitivity = noise(seeds[9], (SUBST, SUBST), SUBST ** -0.5, 1.0, (), jnp.float32)
    return {"coefficients": coefficients, "peak_power": peak_power, "inverter_limit": inverter_limit, "building_feeder": building_feeder, "building_node": building_node, "sky_radiance": sky_radiance, "feeder_nodes": feeder_nodes, "sensitivity": sensitivity, "feeder_substation": feeder_substation, "mv_sensitivity": mv_sensitivity}


def solar_power(coef_rows, peak_rows, limit_rows, sky_table):
    raw_power = jnp.dot(coef_rows, sky_table, preferred_element_type=jnp.float32)
    scaled = raw_power * peak_rows.astype(jnp.float32)[:, None]
    return jnp.minimum(scaled, limit_rows.astype(jnp.float32)[:, None]).astype(jnp.bfloat16)


def reference(coefficients, peak_power, inverter_limit, building_feeder, building_node, sky_radiance, feeder_nodes, sensitivity, feeder_substation, mv_sensitivity):
    power = solar_power(coefficients, peak_power, inverter_limit, sky_radiance)
    target = building_feeder[:, 0].astype(jnp.int32)
    local_node = (building_node % feeder_nodes[target]).astype(jnp.int32)
    flat_index = (target * NODES + local_node).astype(jnp.int32)
    inject = jax.ops.segment_sum(power.astype(jnp.float32), flat_index, num_segments=FEEDERS * NODES)
    inject = inject.reshape(FEEDERS, NODES, COLS)
    head_flow = jnp.sum(inject, axis=1) / (4.0 * B_DEV)
    totals = jax.ops.segment_sum(head_flow, feeder_substation.astype(jnp.int32), num_segments=SUBST)
    medium = jnp.dot(mv_sensitivity, totals, precision=lax.Precision.HIGHEST)
    head_volt = medium[feeder_substation.astype(jnp.int32)]

    def one_feeder(packed):
        matrix, feeder_inject, live_count, base_volt = packed
        rise = jnp.dot(matrix, feeder_inject.astype(jnp.bfloat16), preferred_element_type=jnp.float32)
        live = jnp.arange(NODES, dtype=jnp.int32) < live_count
        return jnp.where(live[:, None], base_volt[None, :] + rise, 0.0).astype(jnp.bfloat16)

    return lax.map(one_feeder, (sensitivity, inject, feeder_nodes, head_volt))
```

```python
import functools

import jax
import jax.numpy as jnp
from jax import lax
from jax.experimental import pallas as pl
from jax.experimental.pallas import tpu as pltpu
from jax.sharding import PartitionSpec as P

MESH = pl.DeviceIdType.MESH
F32 = jnp.float32
BF16 = jnp.bfloat16
I32 = jnp.int32

CAP = 16
WIDE = 256


def nt_dot(a, b):
    return lax.dot_general(a, b, (((1,), (1,)), ((), ())), preferred_element_type=F32)


def iota(shape, axis):
    return lax.broadcasted_iota(I32, shape, axis)


def exchange_kernel(
    regions,
    tiles,
    coef_ref,
    target_ref,
    node_ref,
    peak_ref,
    limit_ref,
    sky_ref,
    live_ref,
    station_ref,
    mv_ref,
    inject_ref,
    base_ref,
    features,
    sky_wide,
    send,
    recv,
    power,
    node_row,
    head,
    heads,
    send_sem,
    recv_sem,
    head_send_sem,
    head_recv_sem,
):
    feeders = regions * tiles
    patches, rows = coef_ref.shape
    columns = sky_ref.shape[1]
    nodes = inject_ref.shape[0]
    slots = feeders * CAP
    my_region, my_tile = lax.axis_index("region"), lax.axis_index("tile")
    me = my_region * tiles + my_tile

    def partner(step):
        region = lax.rem(my_region + step // tiles, regions)
        tile = lax.rem(my_tile + lax.rem(step, tiles), tiles)
        return region, tile

    barrier = pltpu.get_barrier_semaphore()

    def greet(step, carry):
        pl.semaphore_signal(barrier, inc=1, device_id=partner(step), device_id_type=MESH)
        return carry

    lax.fori_loop(1, feeders, greet, 0)

    target = target_ref[...]
    matches = jnp.where(iota((feeders, rows), 0) == target, 1.0, 0.0).astype(F32)
    blocks = rows // 128
    stacked = jnp.concatenate([matches[:, 128 * i : 128 * (i + 1)] for i in range(blocks)], axis=0).astype(BF16)
    left = iota((128, 256), 0) < iota((128, 256), 1)
    counter = jnp.where(left, 1.0, 0.0).astype(BF16)
    counts = jnp.dot(stacked, counter, preferred_element_type=F32)
    carry = jnp.zeros((feeders, 128), F32)
    ranks = []
    for i in range(blocks):
        part = counts[feeders * i : feeders * (i + 1)]
        mine = matches[:, 128 * i : 128 * (i + 1)]
        ranks.append(jnp.sum(mine * (part[:, :128] + carry), axis=0, keepdims=True))
        carry = carry + part[:, 128:]
    rank = jnp.concatenate(ranks, axis=1).astype(I32)
    position = target * CAP + rank

    aligned = patches // 16 * 16
    features[0:aligned, :] = coef_ref[0:aligned, :]
    tail = iota((16, rows), 0)
    raw_node = node_ref[...]
    digits = raw_node // 16
    last = coef_ref[aligned:patches, :].astype(F32)
    extra = jnp.where(tail == 0, jnp.broadcast_to(last, (16, rows)), 0.0)
    extra = jnp.where(tail == 1, peak_ref[...].astype(F32), extra)
    extra = jnp.where(tail == 2, limit_ref[...].astype(F32), extra)
    extra = jnp.where(tail == 3, digits.astype(F32), extra)
    extra = jnp.where(tail == 4, (raw_node - 16 * digits).astype(F32), extra)
    features[aligned : aligned + 16, :] = extra.astype(BF16)
    features[aligned + 16 :, :] = jnp.zeros((WIDE - aligned - 16, rows), BF16)
    sky_wide[0:aligned, :] = sky_ref[0:aligned, :]
    last_sky = jnp.broadcast_to(sky_ref[aligned:patches, :].astype(F32), (16, columns))
    sky_wide[aligned : aligned + 16, :] = jnp.where(iota((16, columns), 0) == 0, last_sky, 0.0).astype(BF16)
    sky_wide[aligned + 16 :, :] = jnp.zeros((WIDE - aligned - 16, columns), BF16)

    chunk = 256
    for i in range(slots // chunk):
        choose = jnp.where(iota((chunk, rows), 0) + chunk * i == position, 1.0, 0.0).astype(BF16)
        packed = nt_dot(choose, features[...]).astype(BF16)
        send[i * (chunk // CAP) : (i + 1) * (chunk // CAP)] = packed.reshape(chunk // CAP, CAP, WIDE)

    pl.semaphore_wait(barrier, feeders - 1)

    own = pltpu.make_async_copy(send.at[me], recv.at[me], recv_sem)
    own.start()

    def ship(step, carry):
        region, tile = partner(step)
        pltpu.make_async_remote_copy(
            src_ref=send.at[region * tiles + tile],
            dst_ref=recv.at[me],
            send_sem=send_sem,
            recv_sem=recv_sem,
            device_id=(region, tile),
            device_id_type=MESH,
        ).start()
        return carry

    lax.fori_loop(1, feeders, ship, 0)
    pltpu.make_async_copy(recv, recv, recv_sem).wait()

    total = jnp.zeros((8, columns), F32)
    for i in range(slots // chunk):
        got = recv[i * (chunk // CAP) : (i + 1) * (chunk // CAP)].reshape(chunk, WIDE)
        raw = jnp.dot(got, sky_wide[...], preferred_element_type=F32)
        peak = got[:, patches : patches + 1].astype(F32)
        limit = got[:, patches + 1 : patches + 2].astype(F32)
        rounded = jnp.minimum(raw * peak, limit).astype(BF16)
        power[i * chunk : (i + 1) * chunk, :] = rounded
        total = total + jnp.sum(rounded.astype(F32).reshape(chunk // 8, 8, columns), axis=0)
    flow = jnp.sum(total, axis=0, keepdims=True) * (1.0 / (4.0 * rows))
    for k in range(columns // 128):
        head[k : k + 1, :] = flow[:, 128 * k : 128 * (k + 1)]
    lanes = columns // 128
    head[lanes:, :] = jnp.full((8 - lanes, 128), station_ref[0], I32).astype(F32)
    own_head = pltpu.make_async_copy(head, heads.at[me], head_recv_sem)
    own_head.start()

    def tell(step, carry):
        pltpu.make_async_remote_copy(
            src_ref=head,
            dst_ref=heads.at[me],
            send_sem=head_send_sem,
            recv_sem=head_recv_sem,
            device_id=partner(step),
            device_id_type=MESH,
        ).start()
        return carry

    lax.fori_loop(1, feeders, tell, 0)

    live = live_ref[0].astype(F32)
    column = iota((8, WIDE), 1)
    weigh = jnp.where(column == patches + 2, 16.0, jnp.where(column == patches + 3, 1.0, 0.0)).astype(BF16)
    raw = nt_dot(weigh, recv[...].reshape(slots, WIDE))[0:1, :]
    node_row[...] = (raw - jnp.floor((raw + 0.5) / live) * live).astype(I32)
    node_block = 512
    for i in range(nodes // node_block):
        hit = jnp.where(iota((node_block, slots), 0) + node_block * i == node_row[...], 1.0, 0.0).astype(BF16)
        inject_ref[node_block * i : node_block * (i + 1), :] = jnp.dot(
            hit, power[...], preferred_element_type=F32
        ).astype(BF16)

    pltpu.make_async_copy(heads, heads, head_recv_sem).wait()
    stations = heads[:, lanes, :]
    picked = jnp.where(stations == iota((feeders, 128), 1).astype(F32), mv_ref[pl.ds(station_ref[0], 1), :], 0.0)
    weight = jnp.sum(picked, axis=1, keepdims=True)
    base_ref[...] = jnp.sum(heads[...] * weight[:, :, None], axis=0)

    def sent(step, carry):
        pltpu.make_async_copy(send.at[0], send.at[0], send_sem).wait()
        pltpu.make_async_copy(head, head, head_send_sem).wait()
        return carry

    lax.fori_loop(1, feeders, sent, 0)


def voltage_kernel(live_ref, matrix_ref, inject_ref, base_ref, out_ref):
    block, columns = out_ref.shape
    base = jnp.concatenate([base_ref[k : k + 1, :] for k in range(columns // 128)], axis=1)
    rise = jnp.dot(matrix_ref[...], inject_ref[...], preferred_element_type=F32)
    row = iota((block, columns), 0) + pl.program_id(0) * block
    out_ref[...] = jnp.where(row < live_ref[0], rise + base, 0.0).astype(BF16)


def on_device(
    regions,
    tiles,
    coefficients,
    peak_power,
    inverter_limit,
    building_feeder,
    building_node,
    sky_radiance,
    feeder_nodes,
    sensitivity,
    feeder_substation,
    mv_sensitivity,
):
    rows = coefficients.shape[0]
    nodes = sensitivity.shape[1]
    columns = sky_radiance.shape[1]
    feeders = regions * tiles
    slots = feeders * CAP
    vmem = pl.BlockSpec(memory_space=pltpu.VMEM)
    smem = pl.BlockSpec(memory_space=pltpu.SMEM)
    mv_wide = jnp.pad(mv_sensitivity, ((0, 0), (0, 128 - mv_sensitivity.shape[1])))
    inject, base = pl.pallas_call(
        functools.partial(exchange_kernel, regions, tiles),
        name="exchange",
        out_shape=(
            jax.ShapeDtypeStruct((nodes, columns), BF16),
            jax.ShapeDtypeStruct((8, 128), F32),
        ),
        in_specs=[vmem] * 6 + [smem] * 2 + [vmem],
        out_specs=(vmem, vmem),
        scratch_shapes=[
            pltpu.VMEM((WIDE, rows), BF16),
            pltpu.VMEM((WIDE, columns), BF16),
            pltpu.VMEM((feeders, CAP, WIDE), BF16),
            pltpu.VMEM((feeders, CAP, WIDE), BF16),
            pltpu.VMEM((slots, columns), BF16),
            pltpu.VMEM((1, slots), I32),
            pltpu.VMEM((8, 128), F32),
            pltpu.VMEM((feeders, 8, 128), F32),
            pltpu.SemaphoreType.DMA,
            pltpu.SemaphoreType.DMA,
            pltpu.SemaphoreType.DMA,
            pltpu.SemaphoreType.DMA,
        ],
        compiler_params=pltpu.CompilerParams(
            collective_id=0, has_side_effects=True, vmem_limit_bytes=48 * 1024 * 1024
        ),
    )(
        coefficients.T,
        building_feeder.reshape(1, rows),
        building_node.reshape(1, rows),
        peak_power.reshape(1, rows),
        inverter_limit.reshape(1, rows),
        sky_radiance,
        feeder_nodes,
        feeder_substation,
        mv_wide,
    )
    block = 512
    voltage = pl.pallas_call(
        voltage_kernel,
        name="voltage",
        grid=(nodes // block,),
        out_shape=jax.ShapeDtypeStruct((nodes, columns), BF16),
        in_specs=[
            smem,
            pl.BlockSpec((block, nodes), lambda i: (i, 0)),
            pl.BlockSpec((nodes, columns), lambda i: (0, 0)),
            pl.BlockSpec((8, 128), lambda i: (0, 0)),
        ],
        out_specs=pl.BlockSpec((block, columns), lambda i: (i, 0)),
        compiler_params=pltpu.CompilerParams(vmem_limit_bytes=40 * 1024 * 1024),
    )(feeder_nodes, sensitivity[0], inject, base)
    return voltage[None, :, :]


def solution(mesh):
    split = P(("region", "tile"))
    return jax.shard_map(
        functools.partial(on_device, mesh.shape["region"], mesh.shape["tile"]),
        mesh=mesh,
        in_specs=(
            P(("region", "tile"), None),
            split,
            split,
            P(("region", "tile"), None),
            split,
            P(),
            split,
            P(("region", "tile"), None, None),
            split,
            P(),
        ),
        out_specs=P(("region", "tile"), None, None),
        check_vma=False,
    )
```
